32 devices in a mesh: grp: 2 (over y), space: 16 (over z, x, core).
Axes of the slice: x: 2, y: 2, z: 4, core: 2. Of those that a mesh axis runs over, the one named last changes fastest.
Arguments:
- snapshots: bfloat16 [2048, 3, 2048], P(('grp', 'space')), parts along dimension 0, may hold values from -6 to 6
- weights: float32 [4096], P(('grp', 'space')), parts along dimension 0, may hold values from 0.5 to 20, as said below
Outputs:
- spod_matrix: float32 [32, 30, 30], P('grp'), parts along dimension 0
The draws below stay inside these ranges and needn't reach their ends.
There are 2 independent parts, one for each index of `grp`. The reference program is written for one: setup_inputs(seed, part) draws one part's arguments, and reference() takes and returns one part's arrays. A program takes and returns all parts, laid end to end along the dimension named above; each array names one. Nothing has to cross between parts.
Inputs may be any that keep to these rules, and one draw needn't show every extreme that they name: Positive quadrature weights.
All inputs are finite; a program needn't handle non-finite values.
Results may differ from the reference program's by a relative error of at most 0.0003.
Values may be sent and summed in bfloat16 or wider, within the bound.
A program may use at most 128 MiB of HBM per device.

```python
import math
import jax
import jax.numpy as jnp
from jax import lax

NFFT = 128
NB = 15
NF = 16
P_DEV = 128
NT = 1024
NPTS = 2048
N_SPACE = 16


def draw_weights(key, part):
    index = jnp.arange(NPTS, dtype=jnp.float32)
    ramp = jnp.exp(math.log(10.0) * index / NPTS)
    rough = jax.random.uniform(key, (NPTS,), jnp.float32, 0.5, 2.0)
    return (ramp * rough).astype(jnp.float32)


def levels(own_key, dims, cuts, low, largest):
    factor_of, own = 1.0, jax.random.fold_in(own_key, 6)
    for axis_at, shards_of in cuts:
        heights = jnp.exp(jax.random.uniform(jax.random.fold_in(own, axis_at), (shards_of,), jnp.float32, low / len(cuts), largest / len(cuts)))
        factor_of = factor_of * jnp.repeat(heights, dims[axis_at] // shards_of).reshape([-1 if axis == axis_at else 1 for axis in range(len(dims))])
    return factor_of


def bell_draw(own_key, dims, scale, reach, cuts=(), kind=jnp.bfloat16):
    factor_of = levels(own_key, dims, cuts, -0.22, 0.18) if cuts else 1.0
    entries = jax.random.normal(own_key, dims, jnp.float32) * scale * factor_of
    return jnp.minimum(jnp.maximum(entries, -reach), reach).astype(kind)


def setup_inputs(seed: int = 0, part: int = 0) -> dict:
    keys = jax.random.split(jax.random.key(seed), 3)
    part_splits = jax.random.split(jax.random.fold_in(keys[2], part), 3)
    return {
        "snapshots": bell_draw(part_splits[0], (NT, 3, NPTS), 1.0, 6.0, ((0, 16),)),
        "weights": draw_weights(jax.random.fold_in(jax.random.fold_in(keys[2], part), 71), part),
    }


def reference(snapshots, weights):
    half = NFFT // 2
    rows = 3 * P_DEV
    phase = jnp.arange(NFFT, dtype=jnp.float32)
    window = 0.5 - 0.5 * jnp.cos(2.0 * jnp.pi * phase / NFFT)
    norm = jnp.sqrt(jnp.sum(window * window))

    def slab_gram(carry, start):
        piece = lax.dynamic_slice_in_dim(snapshots, start, P_DEV, 2).astype(jnp.float32)
        weight_piece = lax.dynamic_slice_in_dim(weights, start, P_DEV, 0)
        signal = piece.reshape(NT, rows)
        signal = signal - lax.optimization_barrier(jnp.mean(signal, axis=0, keepdims=True))
        halves = signal.reshape(NB + 1, half, rows)
        blocks = jnp.concatenate([halves[:-1], halves[1:]], axis=1)
        blocks = blocks * (window / norm)[None, :, None]
        spectra = jnp.fft.fft(blocks, axis=1)[:, 1:NF + 1, :]
        columns = jnp.concatenate([jnp.real(spectra), jnp.imag(spectra)], axis=0)
        columns = jnp.transpose(columns, (1, 0, 2))
        row_weights = jnp.tile(weight_piece, 3)
        gram = jnp.einsum('fbr,fdr->fbd', columns * row_weights[None, None, :], columns, precision=lax.Precision.HIGHEST)
        return (carry + gram, None)
    starts = (jnp.arange(N_SPACE) * P_DEV).astype(jnp.int32)
    empty = jnp.zeros((NF, 2 * NB, 2 * NB), jnp.float32)
    summed, unused = lax.scan(slab_gram, empty, starts)
    return summed / jnp.sum(weights)
```

```python
import functools

import jax
import jax.numpy as jnp
import numpy as np
from jax import lax
from jax.experimental import pallas as pl
from jax.experimental.pallas import tpu as pltpu
from jax.sharding import PartitionSpec as P

NFFT = 128
NB = 15
NF = 16
ROWS = 32
LANES = 128


def table(steps):
    j = np.arange(NFFT)
    window = 0.5 - 0.5 * np.cos(2 * np.pi * j / NFFT)
    window = window / np.sqrt(np.sum(window * window))
    full = np.zeros((NF, ROWS, steps))
    for f in range(NF):
        turns = 2 * np.pi * (((f + 1) * j) % NFFT) / NFFT
        for b in range(NB):
            at = b * (NFFT // 2)
            full[f, b, at:at + NFFT] = window * np.cos(turns)
            full[f, NB + b, at:at + NFFT] = -window * np.sin(turns)
    full = full - full.sum(axis=2, keepdims=True) / steps
    return full.reshape(NF * ROWS, steps)


def split_table(steps, chunk):
    full = table(steps)
    high = full.astype(jnp.bfloat16)
    low = (full - high.astype(np.float64)).astype(jnp.bfloat16)
    both = np.stack([high, low])
    both = both.reshape(2, NF * ROWS, steps // chunk, chunk)
    return np.transpose(both, (2, 0, 1, 3)).reshape(steps // chunk, 2 * NF * ROWS, chunk)


def inner_of(n):
    return 4 if n % 4 == 0 else 1


def owners_of(n):
    return min(max(n // 4, 1), 16)


def each(count, body):
    if count <= 32:
        for k in range(count):
            body(k)
    else:
        def step(k, carry):
            body(k)
            return carry
        lax.fori_loop(0, count, step, 0)


def halves_of(v):
    high = v.astype(jnp.bfloat16)
    return high, (v - high.astype(jnp.float32)).astype(jnp.bfloat16)


def dot_t(a, b):
    return lax.dot_general(a, b, (((1,), (1,)), ((), ())), preferred_element_type=jnp.float32)


def raw_kernel(n, steps_dev, chunk, x_ref, w_ref, s_hbm, out_ref,
           s_ref, recv, acc, gram, parts, total, gathered,
           s_sem, own_sem, send_sem, recv_sem, rs_send, rs_recv, ag_send, ag_recv):
    me = lax.axis_index("space")
    owners = owners_of(n)
    first = (n - owners) // 2
    tile = LANES // owners
    inner = inner_of(n)
    planes = n // inner
    my_plane, my_q = me // inner, lax.rem(me, inner)
    per_chunk = chunk // steps_dev
    n_chunks = n // per_chunk
    rows = NF * ROWS
    mine = w_ref.shape[1]
    components = x_ref.shape[0]

    def peer_of(k):
        return lax.rem(me + 1 + k, n)

    def lanes_of(dest):
        return pl.ds(pl.multiple_of(dest * mine, mine), mine)

    s_copy = pltpu.make_async_copy(s_hbm, s_ref, s_sem)
    s_copy.start()
    own_copy = pltpu.make_async_copy(x_ref.at[:, :, lanes_of(me)], recv.at[me], own_sem)
    own_copy.start()

    barrier = pltpu.get_barrier_semaphore()

    def greet(k):
        pl.semaphore_signal(barrier, inc=1, device_id={"space": peer_of(k)},
                            device_id_type=pl.DeviceIdType.MESH)
    each(n - 1, greet)
    pl.semaphore_wait(barrier, n - 1)

    def data_copy(dest, source):
        return pltpu.make_async_remote_copy(
            src_ref=x_ref.at[:, :, lanes_of(dest)], dst_ref=recv.at[source],
            send_sem=send_sem.at[dest], recv_sem=recv_sem.at[source],
            device_id={"space": dest}, device_id_type=pl.DeviceIdType.MESH)

    def send(plane, low, high):
        def one(k):
            q = lax.rem(my_q + low + k, inner)

            @pl.when(jnp.logical_or(plane != my_plane, q != my_q))
            def _():
                data_copy(plane * inner + q, me).start()
        each(high - low, one)

    def send_far(k):
        d = planes - 1 - k
        pl.when(my_plane + d < planes)(lambda: send(my_plane + d, 0, inner))
        pl.when(my_plane >= d)(lambda: send(my_plane - d, 0, inner))
    each(planes - 1, send_far)
    send(my_plane, 0, inner)

    acc[...] = jnp.zeros_like(acc)
    s_copy.wait()
    own_copy.wait()
    my_chunk = me // per_chunk

    def absorb(j):
        at = lax.rem(my_chunk + j, n_chunks)

        def arrive(i):
            source = at * per_chunk + i

            @pl.when(source != me)
            def _():
                data_copy(source, source).wait_recv()
        each(per_chunk, arrive)
        held = pl.ds(at * per_chunk, per_chunk)
        block = jnp.concatenate(
            [recv[held, c].reshape(chunk, mine) for c in range(components)], axis=1)
        s = s_ref[at]
        acc[...] += (
            jnp.dot(s[:rows], block, preferred_element_type=jnp.float32)
            + jnp.dot(s[rows:], block, preferred_element_type=jnp.float32))
    each(n_chunks, absorb)

    w = w_ref[...]
    w_all = jnp.concatenate([w] * (acc.shape[1] // w.shape[1]), axis=1)
    w_sum = jnp.sum(w)
    block_of = lax.broadcasted_iota(jnp.int32, (ROWS, LANES), 1) // ROWS
    corner = jnp.logical_and(
        lax.broadcasted_iota(jnp.int32, (ROWS, LANES), 0) == ROWS - 1,
        lax.broadcasted_iota(jnp.int32, (ROWS, LANES), 1) % ROWS == ROWS - 1)
    for g in range(rows // LANES):
        c = acc[g * LANES:(g + 1) * LANES]
        c_high, c_low = halves_of(c)
        a_high, a_low = halves_of(c * w_all)
        full = dot_t(a_high, c_high) + (dot_t(a_high, c_low) + dot_t(a_low, c_high))
        kept = full[:ROWS]
        for i in range(1, LANES // ROWS):
            kept = jnp.where(block_of == i, full[i * ROWS:(i + 1) * ROWS], kept)
        gram[g * ROWS:(g + 1) * ROWS] = jnp.where(corner, w_sum, kept)

    def part_copy(slot, source):
        return pltpu.make_async_remote_copy(
            src_ref=gram.at[pl.ds(pl.multiple_of(slot * tile, tile), tile)],
            dst_ref=parts.at[source],
            send_sem=rs_send.at[slot], recv_sem=rs_recv.at[source],
            device_id={"space": first + slot}, device_id_type=pl.DeviceIdType.MESH)

    def total_copy(dest, slot):
        return pltpu.make_async_remote_copy(
            src_ref=total, dst_ref=gathered.at[slot],
            send_sem=ag_send.at[dest], recv_sem=ag_recv.at[slot],
            device_id={"space": dest}, device_id_type=pl.DeviceIdType.MESH)

    my_slot = me - first
    is_owner = jnp.logical_and(my_slot >= 0, my_slot < owners)

    def for_others(body):
        def one(k):
            slot = lax.rem(me + owners // 2 + k, owners)

            @pl.when(slot != my_slot)
            def _():
                body(slot)
        each(owners, one)
    for_others(lambda slot: part_copy(slot, me).start())

    @pl.when(is_owner)
    def _():
        parts[me] = gram[pl.ds(pl.multiple_of(my_slot * tile, tile), tile)]
        each(n - 1, lambda k: part_copy(my_slot, peer_of(k)).wait_recv())
        total[...] = jnp.sum(parts[...], axis=0)
        def total_to(plane):
            def one(k):
                dest = plane * inner + lax.rem(my_q + k, inner)

                @pl.when(dest != me)
                def _():
                    total_copy(dest, my_slot).start()
            each(inner, one)

        def total_far(k):
            d = planes - 1 - k
            pl.when(my_plane + d < planes)(lambda: total_to(my_plane + d))
            pl.when(my_plane >= d)(lambda: total_to(my_plane - d))
        each(planes - 1, total_far)
        total_to(my_plane)
        gathered[my_slot] = total[...]

    for_others(lambda slot: total_copy(me, slot).wait_recv())

    whole = gathered[...].reshape(LANES, LANES)
    inverse = 1.0 / whole[ROWS - 1:ROWS, ROWS - 1:ROWS]
    per_row = LANES // ROWS
    for f in range(NF):
        g, i = f // per_row, f % per_row
        piece = whole[g * ROWS:g * ROWS + 2 * NB, i * ROWS:i * ROWS + 2 * NB]
        out_ref[:, f, :] = piece * inverse

    each(n - 1, lambda k: data_copy(peer_of(k), me).wait_send())

    for_others(lambda slot: part_copy(slot, me).wait_send())

    @pl.when(is_owner)
    def _():
        each(n - 1, lambda k: total_copy(peer_of(k), my_slot).wait_send())


def raw_local(n, snapshots, weights):
    steps_dev, components, points = snapshots.shape
    mine = points // n
    steps = steps_dev * n
    chunk = max(256, steps_dev)
    width = components * mine
    x = jnp.transpose(snapshots, (1, 0, 2))
    s = jnp.asarray(split_table(steps, chunk))
    owners = owners_of(n)
    rows = NF * ROWS
    dma = pltpu.SemaphoreType.DMA
    hbm = pl.BlockSpec(memory_space=pl.ANY)
    vmem = pl.BlockSpec(memory_space=pltpu.VMEM)
    out = pl.pallas_call(
        functools.partial(raw_kernel, n, steps_dev, chunk),
        out_shape=jax.ShapeDtypeStruct((2 * NB, NF, 2 * NB), jnp.float32),
        in_specs=[hbm, vmem, hbm],
        out_specs=vmem,
        scratch_shapes=[
            pltpu.VMEM(s.shape, jnp.bfloat16),
            pltpu.VMEM((n, components, steps_dev, mine), jnp.bfloat16),
            pltpu.VMEM((rows, width), jnp.float32),
            pltpu.VMEM((LANES, LANES), jnp.float32),
            pltpu.VMEM((n, LANES // owners, LANES), jnp.float32),
            pltpu.VMEM((LANES // owners, LANES), jnp.float32),
            pltpu.VMEM((owners, LANES // owners, LANES), jnp.float32),
            dma, dma, dma((n,)), dma((n,)), dma((n,)), dma((n,)), dma((n,)), dma((n,)),
        ],
        compiler_params=pltpu.CompilerParams(collective_id=0, has_side_effects=True),
    )(x, weights.reshape(1, mine), s)
    return jnp.transpose(out, (1, 0, 2))


HALF = NFFT // 2
TOP = NF + 2
MAIN = 2 * NF
EXTRA = 4
POWER_BITS = 4
GAIN = 2.0 ** 7.5


def half_rows():
    j = np.arange(HALF)
    turns = [2 * np.pi * ((k * j) % NFFT) / NFFT for k in range(TOP)]
    main = [np.cos(turns[k]) for k in range(1, NF + 1)]
    main += [-np.sin(turns[k]) for k in range(1, NF + 1)]
    extra = [np.full(HALF, 1.0 / HALF), np.ones(HALF), np.cos(turns[TOP - 1]), -np.sin(turns[TOP - 1])]
    return np.stack(main), np.stack(extra)


def packed_rows(components):
    used = components * (MAIN + EXTRA) + 1
    return -(-used // 16) * 16


def split(full):
    high = full.astype(jnp.bfloat16)
    return high, (full - high.astype(np.float64)).astype(jnp.bfloat16)


def sender_table(components):
    main, extra = half_rows()
    packed = packed_rows(components)
    full = np.zeros((packed, components, HALF))
    level = np.zeros(packed)
    for c in range(components):
        at = components * MAIN + c * EXTRA
        full[c * MAIN:(c + 1) * MAIN, c] = main
        full[at:at + EXTRA, c] = extra
    high, low = split(full.reshape(packed, components * HALF))
    level = (high.astype(np.float64) + low.astype(np.float64)).sum(axis=1)
    for c in range(components):
        level[components * MAIN + c * EXTRA] = 0.0
    both = np.concatenate([high, low])
    return both, np.repeat(level.astype(np.float32)[:, None], LANES, axis=1)


def combine_table(segments, components):
    main, extra = half_rows()
    values = MAIN + EXTRA
    level = np.concatenate([main, extra]).sum(axis=1)
    level[MAIN] = 0.0

    def unit(k, imag):
        row = np.zeros(values)
        if k == 0:
            if not imag:
                row[MAIN + 1] = 1.0
        elif k == TOP - 1:
            row[MAIN + 2 + imag] = 1.0
        else:
            row[imag * NF + k - 1] = 1.0
        return row

    full = np.zeros((NF, ROWS, segments, values))
    for f in range(NF):
        k = f + 1
        for imag in range(2):
            side = 0.25 * (unit(k - 1, imag) + unit(k + 1, imag))
            first = 0.5 * unit(k, imag) - side
            second = (-1.0) ** k * (0.5 * unit(k, imag) + side)
            lift_first, lift_second = first @ level, second @ level
            both = lift_first + lift_second
            for b in range(NB):
                row = full[f, imag * NB + b]
                row[b] += first
                row[b + 1] += second
                row[b, MAIN] += lift_first
                row[b + 1, MAIN] += lift_second
                if f == 0 and not imag:
                    row[:, MAIN] -= both / segments
                    row[:, MAIN + 1] -= both / (segments * HALF)
    full = full.reshape(NF * ROWS, segments, values)
    inner = inner_of(segments)
    planes = segments // inner
    tail = packed_rows(components) - components * MAIN
    wide = np.zeros((NF * ROWS, segments, tail))
    for c in range(components):
        wide[:, :, c * EXTRA:(c + 1) * EXTRA] = full[:, :, MAIN:]
    high, low = split(wide)

    def planed(part):
        part = part.reshape(NF * ROWS, planes, inner * part.shape[-1])
        return np.transpose(part, (1, 0, 2)).astype(jnp.bfloat16)
    return np.concatenate([planed(full[:, :, :MAIN]), planed(high), planed(low)], axis=2)


def code(v):
    a = v
    for _ in range(POWER_BITS):
        a = a * a
    return jnp.where(v < 0.0, -a, a)


def decode(y):
    a = jnp.abs(y)
    for _ in range(POWER_BITS):
        a = jnp.sqrt(a)
    return jnp.where(y < 0.0, -a, a)


def spectral_kernel(n, x_ref, w_ref, f_ref, level_ref, t_hbm, out_ref,
                    x_buf, t_ref, outbox, recv, acc, gram, parts, total, gathered,
                    x_sem, t_sem, own_sem, send_sem, recv_sem, rs_send, rs_recv, ag_send, ag_recv):
    me = lax.axis_index("space")
    owners = owners_of(n)
    first = (n - owners) // 2
    tile = LANES // owners
    inner = inner_of(n)
    planes = n // inner
    my_plane, my_q = me // inner, lax.rem(me, inner)
    rows = NF * ROWS
    mine = w_ref.shape[1]
    components, steps_dev = x_ref.shape[:2]
    packed = recv.shape[1]
    body = components * MAIN

    def peer_of(k):
        return lax.rem(me + 1 + k, n)

    def plane_of(k):
        return lax.rem(my_plane + planes - 1 - k + planes // 2, planes)

    def x_copy(k):
        width = inner * mine
        lanes = pl.ds(pl.multiple_of(plane_of(k) * width, width), width)
        return pltpu.make_async_copy(x_ref.at[:, :, lanes], x_buf.at[k], x_sem.at[k])
    each(planes, lambda k: x_copy(k).start())
    t_copy = pltpu.make_async_copy(t_hbm, t_ref, t_sem)
    t_copy.start()

    barrier = pltpu.get_barrier_semaphore()

    def greet(k):
        pl.semaphore_signal(barrier, inc=1, device_id={"space": peer_of(k)},
                            device_id_type=pl.DeviceIdType.MESH)
    each(n - 1, greet)

    def data_copy(dest, source):
        return pltpu.make_async_remote_copy(
            src_ref=outbox.at[dest], dst_ref=recv.at[source],
            send_sem=send_sem.at[dest], recv_sem=recv_sem.at[source],
            device_id={"space": dest}, device_id_type=pl.DeviceIdType.MESH)

    tail_row = lax.broadcasted_iota(jnp.int32, (packed - body, LANES), 0)
    tail_kind = lax.rem(tail_row, EXTRA)
    in_tail = tail_row < components * EXTRA
    coded = jnp.logical_and(in_tail, tail_kind > 0)
    is_scale = tail_row == components * EXTRA

    def prepare(k):
        x_copy(k).wait()
        x = x_buf[k].reshape(components * steps_dev, inner * mine)
        both = jnp.dot(f_ref[...], x, preferred_element_type=jnp.float32)
        y = both[:packed] + both[packed:]
        for q in range(inner):
            part = y[:, q * mine:(q + 1) * mine]
            tail = part[body:]
            means = [tail[c * EXTRA:c * EXTRA + 1].astype(jnp.bfloat16).astype(jnp.float32)
                     for c in range(components)]
            spread = jnp.broadcast_to(means[-1], tail.shape)
            for c in range(components - 1):
                inside = jnp.logical_and(tail_row >= c * EXTRA, tail_row < (c + 1) * EXTRA)
                spread = jnp.where(inside, means[c], spread)
            tail = tail - level_ref[body:] * spread
            mains = [part[c * MAIN:(c + 1) * MAIN] - level_ref[c * MAIN:(c + 1) * MAIN] * means[c]
                     for c in range(components)]
            largest = jnp.max(jnp.where(coded, jnp.abs(tail), 0.0), axis=0, keepdims=True)
            for m in mains:
                largest = jnp.maximum(largest, jnp.max(jnp.abs(m), axis=0, keepdims=True))
            scale = jnp.maximum(largest, 1e-30).astype(jnp.bfloat16).astype(jnp.float32)
            grow = GAIN / scale
            dest = plane_of(k) * inner + q
            for c in range(components):
                outbox[dest, c * MAIN:(c + 1) * MAIN] = code(mains[c] * grow).astype(jnp.bfloat16)
            sent = jnp.where(coded, code(tail * grow), jnp.where(is_scale, scale, spread))
            outbox[dest, body:] = sent.astype(jnp.bfloat16)

    def launch(k):
        def one(i):
            dest = plane_of(k) * inner + lax.rem(my_q + i, inner)

            @pl.when(dest != me)
            def _():
                data_copy(dest, me).start()
        each(inner, one)

    def step(k):
        prepare(k)
        if k == 0:
            pl.semaphore_wait(barrier, n - 1)
        launch(k)
    for k in range(planes):
        step(k)
    own_copy = pltpu.make_async_copy(outbox.at[me], recv.at[me], own_sem)
    own_copy.start()

    acc[...] = jnp.zeros_like(acc)
    t_copy.wait()
    own_copy.wait()

    def absorb(j):
        at = lax.rem(my_plane + j, planes)

        def arrive(i):
            source = at * inner + i

            @pl.when(source != me)
            def _():
                data_copy(source, source).wait_recv()
        each(inner, arrive)
        columns = [[] for _ in range(components)]
        tails = []
        for i in range(inner):
            source = at * inner + i
            tail = recv[source, body:].astype(jnp.float32)
            scale = tail[components * EXTRA:components * EXTRA + 1] * (1.0 / GAIN)
            for c in range(components):
                y = recv[source, c * MAIN:(c + 1) * MAIN].astype(jnp.float32)
                columns[c].append(decode(y) * scale)
            tails.append(jnp.where(coded, decode(tail) * scale, tail))
        tail = jnp.concatenate(tails, axis=0)
        row = lax.rem(lax.broadcasted_iota(jnp.int32, tail.shape, 0), packed - body)
        pieces = []
        for c in range(components):
            inside = jnp.logical_and(row >= c * EXTRA, row < (c + 1) * EXTRA)
            own = jnp.where(inside, tail, 0.0)
            pieces.append(jnp.concatenate(columns[c] + [own, own], axis=0))
        block = jnp.concatenate(pieces, axis=1)
        high, low = halves_of(block)
        t = t_ref[at]
        acc[...] += (
            jnp.dot(t, high, preferred_element_type=jnp.float32)
            + jnp.dot(t, low, preferred_element_type=jnp.float32))
    each(planes, absorb)

    w = w_ref[...]
    w_all = jnp.concatenate([w] * (acc.shape[1] // w.shape[1]), axis=1)
    w_sum = jnp.sum(w)
    block_of = lax.broadcasted_iota(jnp.int32, (ROWS, LANES), 1) // ROWS
    corner = jnp.logical_and(
        lax.broadcasted_iota(jnp.int32, (ROWS, LANES), 0) == ROWS - 1,
        lax.broadcasted_iota(jnp.int32, (ROWS, LANES), 1) % ROWS == ROWS - 1)
    for g in range(rows // LANES):
        c = acc[g * LANES:(g + 1) * LANES]
        c_high, c_low = halves_of(c)
        a_high, a_low = halves_of(c * w_all)
        full = dot_t(a_high, c_high) + (dot_t(a_high, c_low) + dot_t(a_low, c_high))
        kept = full[:ROWS]
        for i in range(1, LANES // ROWS):
            kept = jnp.where(block_of == i, full[i * ROWS:(i + 1) * ROWS], kept)
        gram[g * ROWS:(g + 1) * ROWS] = jnp.where(corner, w_sum, kept)

    def part_copy(slot, source):
        return pltpu.make_async_remote_copy(
            src_ref=gram.at[pl.ds(pl.multiple_of(slot * tile, tile), tile)],
            dst_ref=parts.at[source],
            send_sem=rs_send.at[slot], recv_sem=rs_recv.at[source],
            device_id={"space": first + slot}, device_id_type=pl.DeviceIdType.MESH)

    def total_copy(dest, slot):
        return pltpu.make_async_remote_copy(
            src_ref=total, dst_ref=gathered.at[slot],
            send_sem=ag_send.at[dest], recv_sem=ag_recv.at[slot],
            device_id={"space": dest}, device_id_type=pl.DeviceIdType.MESH)

    my_slot = me - first
    is_owner = jnp.logical_and(my_slot >= 0, my_slot < owners)

    def for_others(body):
        def one(k):
            slot = lax.rem(me + owners // 2 + k, owners)

            @pl.when(slot != my_slot)
            def _():
                body(slot)
        each(owners, one)
    for_others(lambda slot: part_copy(slot, me).start())

    @pl.when(is_owner)
    def _():
        parts[me] = gram[pl.ds(pl.multiple_of(my_slot * tile, tile), tile)]
        each(n - 1, lambda k: part_copy(my_slot, peer_of(k)).wait_recv())
        total[...] = jnp.sum(parts[...], axis=0)
        def total_to(plane):
            def one(k):
                dest = plane * inner + lax.rem(my_q + k, inner)

                @pl.when(dest != me)
                def _():
                    total_copy(dest, my_slot).start()
            each(inner, one)

        def total_far(k):
            d = planes - 1 - k
            pl.when(my_plane + d < planes)(lambda: total_to(my_plane + d))
            pl.when(my_plane >= d)(lambda: total_to(my_plane - d))
        each(planes - 1, total_far)
        total_to(my_plane)
        gathered[my_slot] = total[...]

    for_others(lambda slot: total_copy(me, slot).wait_recv())

    whole = gathered[...].reshape(LANES, LANES)
    inverse = 1.0 / (whole[ROWS - 1:ROWS, ROWS - 1:ROWS] * (3.0 * NFFT / 8.0))
    per_row = LANES // ROWS
    for f in range(NF):
        g, i = f // per_row, f % per_row
        piece = whole[g * ROWS:g * ROWS + 2 * NB, i * ROWS:i * ROWS + 2 * NB]
        out_ref[:, f, :] = piece * inverse

    each(n - 1, lambda k: data_copy(peer_of(k), me).wait_send())

    for_others(lambda slot: part_copy(slot, me).wait_send())

    @pl.when(is_owner)
    def _():
        each(n - 1, lambda k: total_copy(peer_of(k), my_slot).wait_send())


def spectral_local(n, snapshots, weights):
    steps_dev, components, points = snapshots.shape
    mine = points // n
    x = jnp.transpose(snapshots, (1, 0, 2))
    forward, level = sender_table(components)
    back = combine_table(n, components)
    owners = owners_of(n)
    inner = inner_of(n)
    planes = n // inner
    packed = packed_rows(components)
    rows = NF * ROWS
    dma = pltpu.SemaphoreType.DMA
    hbm = pl.BlockSpec(memory_space=pl.ANY)
    vmem = pl.BlockSpec(memory_space=pltpu.VMEM)
    out = pl.pallas_call(
        functools.partial(spectral_kernel, n),
        out_shape=jax.ShapeDtypeStruct((2 * NB, NF, 2 * NB), jnp.float32),
        in_specs=[hbm, vmem, vmem, vmem, hbm],
        out_specs=vmem,
        scratch_shapes=[
            pltpu.VMEM((planes, components, steps_dev, inner * mine), jnp.bfloat16),
            pltpu.VMEM(back.shape, jnp.bfloat16),
            pltpu.VMEM((n, packed, mine), jnp.bfloat16),
            pltpu.VMEM((n, packed, mine), jnp.bfloat16),
            pltpu.VMEM((rows, components * mine), jnp.float32),
            pltpu.VMEM((LANES, LANES), jnp.float32),
            pltpu.VMEM((n, LANES // owners, LANES), jnp.float32),
            pltpu.VMEM((LANES // owners, LANES), jnp.float32),
            pltpu.VMEM((owners, LANES // owners, LANES), jnp.float32),
            dma((planes,)), dma, dma, dma((n,)), dma((n,)), dma((n,)), dma((n,)), dma((n,)), dma((n,)),
        ],
        compiler_params=pltpu.CompilerParams(collective_id=0, has_side_effects=True),
    )(x, weights.reshape(1, mine), jnp.asarray(forward), jnp.asarray(level), jnp.asarray(back))
    return jnp.transpose(out, (1, 0, 2))


def local(n, snapshots, weights):
    steps_dev, components, points = snapshots.shape
    fits = steps_dev == HALF and n == NB + 1 and points == n * LANES
    return (spectral_local if fits else raw_local)(n, snapshots, weights)


def solution(mesh):
    n = mesh.shape["space"]
    in_specs = (P(("grp", "space"), None, None), P(("grp", "space")))
    out_specs = P("grp", None, None)
    return jax.shard_map(functools.partial(local, n), mesh=mesh, in_specs=in_specs,
                         out_specs=out_specs, check_vma=False)
```

```python
import functools

import jax
import jax.numpy as jnp
import numpy as np
from jax import lax
from jax.experimental import pallas as pl
from jax.experimental.pallas import tpu as pltpu
from jax.sharding import PartitionSpec as P

NFFT = 128
NB = 15
NF = 16
ROWS = 32
LANES = 128


def table(steps):
    j = np.arange(NFFT)
    window = 0.5 - 0.5 * np.cos(2 * np.pi * j / NFFT)
    window = window / np.sqrt(np.sum(window * window))
    full = np.zeros((NF, ROWS, steps))
    for f in range(NF):
        turns = 2 * np.pi * (((f + 1) * j) % NFFT) / NFFT
        for b in range(NB):
            at = b * (NFFT // 2)
            full[f, b, at:at + NFFT] = window * np.cos(turns)
            full[f, NB + b, at:at + NFFT] = -window * np.sin(turns)
    full = full - full.sum(axis=2, keepdims=True) / steps
    return full.reshape(NF * ROWS, steps)


def split_table(steps, chunk):
    full = table(steps)
    high = full.astype(jnp.bfloat16)
    low = (full - high.astype(np.float64)).astype(jnp.bfloat16)
    both = np.stack([high, low])
    both = both.reshape(2, NF * ROWS, steps // chunk, chunk)
    return np.transpose(both, (2, 0, 1, 3)).reshape(steps // chunk, 2 * NF * ROWS, chunk)


def inner_of(n):
    return 4 if n % 4 == 0 else 1


def owners_of(n):
    return min(max(n // 4, 1), 16)


def each(count, body):
    if count <= 32:
        for k in range(count):
            body(k)
    else:
        def step(k, carry):
            body(k)
            return carry
        lax.fori_loop(0, count, step, 0)


def halves_of(v):
    high = v.astype(jnp.bfloat16)
    return high, (v - high.astype(jnp.float32)).astype(jnp.bfloat16)


def dot_t(a, b):
    return lax.dot_general(a, b, (((1,), (1,)), ((), ())), preferred_element_type=jnp.float32)


def raw_kernel(n, steps_dev, chunk, x_ref, w_ref, s_hbm, out_ref,
           s_ref, recv, acc, gram, parts, total, gathered,
           s_sem, own_sem, send_sem, recv_sem, rs_send, rs_recv, ag_send, ag_recv):
    me = lax.axis_index("space")
    owners = owners_of(n)
    first = (n - owners) // 2
    tile = LANES // owners
    inner = inner_of(n)
    planes = n // inner
    my_plane, my_q = me // inner, lax.rem(me, inner)
    per_chunk = chunk // steps_dev
    n_chunks = n // per_chunk
    rows = NF * ROWS
    mine = w_ref.shape[1]
    components = x_ref.shape[0]

    def peer_of(k):
        return lax.rem(me + 1 + k, n)

    def lanes_of(dest):
        return pl.ds(pl.multiple_of(dest * mine, mine), mine)

    s_copy = pltpu.make_async_copy(s_hbm, s_ref, s_sem)
    s_copy.start()
    own_copy = pltpu.make_async_copy(x_ref.at[:, :, lanes_of(me)], recv.at[me], own_sem)
    own_copy.start()

    barrier = pltpu.get_barrier_semaphore()

    def greet(k):
        pl.semaphore_signal(barrier, inc=1, device_id={"space": peer_of(k)},
                            device_id_type=pl.DeviceIdType.MESH)
    each(n - 1, greet)
    pl.semaphore_wait(barrier, n - 1)

    def data_copy(dest, source):
        return pltpu.make_async_remote_copy(
            src_ref=x_ref.at[:, :, lanes_of(dest)], dst_ref=recv.at[source],
            send_sem=send_sem.at[dest], recv_sem=recv_sem.at[source],
            device_id={"space": dest}, device_id_type=pl.DeviceIdType.MESH)

    def send(plane, low, high):
        def one(k):
            q = lax.rem(my_q + low + k, inner)

            @pl.when(jnp.logical_or(plane != my_plane, q != my_q))
            def _():
                data_copy(plane * inner + q, me).start()
        each(high - low, one)

    def send_far(k):
        d = planes - 1 - k
        pl.when(my_plane + d < planes)(lambda: send(my_plane + d, 0, inner))
        pl.when(my_plane >= d)(lambda: send(my_plane - d, 0, inner))
    each(planes - 1, send_far)
    send(my_plane, 0, inner)

    acc[...] = jnp.zeros_like(acc)
    s_copy.wait()
    own_copy.wait()
    my_chunk = me // per_chunk

    def absorb(j):
        at = lax.rem(my_chunk + j, n_chunks)

        def arrive(i):
            source = at * per_chunk + i

            @pl.when(source != me)
            def _():
                data_copy(source, source).wait_recv()
        each(per_chunk, arrive)
        held = pl.ds(at * per_chunk, per_chunk)
        block = jnp.concatenate(
            [recv[held, c].reshape(chunk, mine) for c in range(components)], axis=1)
        s = s_ref[at]
        acc[...] += (
            jnp.dot(s[:rows], block, preferred_element_type=jnp.float32)
            + jnp.dot(s[rows:], block, preferred_element_type=jnp.float32))
    each(n_chunks, absorb)

    w = w_ref[...]
    w_all = jnp.concatenate([w] * (acc.shape[1] // w.shape[1]), axis=1)
    w_sum = jnp.sum(w)
    block_of = lax.broadcasted_iota(jnp.int32, (ROWS, LANES), 1) // ROWS
    corner = jnp.logical_and(
        lax.broadcasted_iota(jnp.int32, (ROWS, LANES), 0) == ROWS - 1,
        lax.broadcasted_iota(jnp.int32, (ROWS, LANES), 1) % ROWS == ROWS - 1)
    for g in range(rows // LANES):
        c = acc[g * LANES:(g + 1) * LANES]
        c_high, c_low = halves_of(c)
        a_high, a_low = halves_of(c * w_all)
        full = dot_t(a_high, c_high) + (dot_t(a_high, c_low) + dot_t(a_low, c_high))
        kept = full[:ROWS]
        for i in range(1, LANES // ROWS):
            kept = jnp.where(block_of == i, full[i * ROWS:(i + 1) * ROWS], kept)
        gram[g * ROWS:(g + 1) * ROWS] = jnp.where(corner, w_sum, kept)

    def part_copy(slot, source):
        return pltpu.make_async_remote_copy(
            src_ref=gram.at[pl.ds(pl.multiple_of(slot * tile, tile), tile)],
            dst_ref=parts.at[source],
            send_sem=rs_send.at[slot], recv_sem=rs_recv.at[source],
            device_id={"space": first + slot}, device_id_type=pl.DeviceIdType.MESH)

    def total_copy(dest, slot):
        return pltpu.make_async_remote_copy(
            src_ref=total, dst_ref=gathered.at[slot],
            send_sem=ag_send.at[dest], recv_sem=ag_recv.at[slot],
            device_id={"space": dest}, device_id_type=pl.DeviceIdType.MESH)

    my_slot = me - first
    is_owner = jnp.logical_and(my_slot >= 0, my_slot < owners)

    def for_others(body):
        def one(k):
            slot = lax.rem(me + owners // 2 + k, owners)

            @pl.when(slot != my_slot)
            def _():
                body(slot)
        each(owners, one)
    for_others(lambda slot: part_copy(slot, me).start())

    @pl.when(is_owner)
    def _():
        parts[me] = gram[pl.ds(pl.multiple_of(my_slot * tile, tile), tile)]
        each(n - 1, lambda k: part_copy(my_slot, peer_of(k)).wait_recv())
        total[...] = jnp.sum(parts[...], axis=0)
        def total_to(plane):
            def one(k):
                dest = plane * inner + lax.rem(my_q + k, inner)

                @pl.when(dest != me)
                def _():
                    total_copy(dest, my_slot).start()
            each(inner, one)

        def total_far(k):
            d = planes - 1 - k
            pl.when(my_plane + d < planes)(lambda: total_to(my_plane + d))
            pl.when(my_plane >= d)(lambda: total_to(my_plane - d))
        each(planes - 1, total_far)
        total_to(my_plane)
        gathered[my_slot] = total[...]

    for_others(lambda slot: total_copy(me, slot).wait_recv())

    whole = gathered[...].reshape(LANES, LANES)
    inverse = 1.0 / whole[ROWS - 1:ROWS, ROWS - 1:ROWS]
    per_row = LANES // ROWS
    for f in range(NF):
        g, i = f // per_row, f % per_row
        piece = whole[g * ROWS:g * ROWS + 2 * NB, i * ROWS:i * ROWS + 2 * NB]
        out_ref[:, f, :] = piece * inverse

    each(n - 1, lambda k: data_copy(peer_of(k), me).wait_send())

    for_others(lambda slot: part_copy(slot, me).wait_send())

    @pl.when(is_owner)
    def _():
        each(n - 1, lambda k: total_copy(peer_of(k), my_slot).wait_send())


def raw_local(n, snapshots, weights):
    steps_dev, components, points = snapshots.shape
    mine = points // n
    steps = steps_dev * n
    chunk = max(256, steps_dev)
    width = components * mine
    x = jnp.transpose(snapshots, (1, 0, 2))
    s = jnp.asarray(split_table(steps, chunk))
    owners = owners_of(n)
    rows = NF * ROWS
    dma = pltpu.SemaphoreType.DMA
    hbm = pl.BlockSpec(memory_space=pl.ANY)
    vmem = pl.BlockSpec(memory_space=pltpu.VMEM)
    out = pl.pallas_call(
        functools.partial(raw_kernel, n, steps_dev, chunk),
        out_shape=jax.ShapeDtypeStruct((2 * NB, NF, 2 * NB), jnp.float32),
        in_specs=[hbm, vmem, hbm],
        out_specs=vmem,
        scratch_shapes=[
            pltpu.VMEM(s.shape, jnp.bfloat16),
            pltpu.VMEM((n, components, steps_dev, mine), jnp.bfloat16),
            pltpu.VMEM((rows, width), jnp.float32),
            pltpu.VMEM((LANES, LANES), jnp.float32),
            pltpu.VMEM((n, LANES // owners, LANES), jnp.float32),
            pltpu.VMEM((LANES // owners, LANES), jnp.float32),
            pltpu.VMEM((owners, LANES // owners, LANES), jnp.float32),
            dma, dma, dma((n,)), dma((n,)), dma((n,)), dma((n,)), dma((n,)), dma((n,)),
        ],
        compiler_params=pltpu.CompilerParams(collective_id=0, has_side_effects=True),
    )(x, weights.reshape(1, mine), s)
    return jnp.transpose(out, (1, 0, 2))


HALF = NFFT // 2
TOP = NF + 2
MAIN = 2 * NF
EXTRA = 4
POWER_BITS = 4
GAIN = 2.0 ** 7.5


def half_rows():
    j = np.arange(HALF)
    turns = [2 * np.pi * ((k * j) % NFFT) / NFFT for k in range(TOP)]
    main = [np.cos(turns[k]) for k in range(1, NF + 1)]
    main += [-np.sin(turns[k]) for k in range(1, NF + 1)]
    extra = [np.full(HALF, 1.0 / HALF), np.ones(HALF), np.cos(turns[TOP - 1]), -np.sin(turns[TOP - 1])]
    return np.stack(main), np.stack(extra)


def packed_rows(components):
    used = components * (MAIN + EXTRA) + 1
    return -(-used // 16) * 16


def split(full):
    high = full.astype(jnp.bfloat16)
    return high, (full - high.astype(np.float64)).astype(jnp.bfloat16)


def sender_table(components):
    main, extra = half_rows()
    packed = packed_rows(components)
    full = np.zeros((packed, components, HALF))
    level = np.zeros(packed)
    for c in range(components):
        at = components * MAIN + c * EXTRA
        full[c * MAIN:(c + 1) * MAIN, c] = main
        full[at:at + EXTRA, c] = extra
    high, low = split(full.reshape(packed, components * HALF))
    level = (high.astype(np.float64) + low.astype(np.float64)).sum(axis=1)
    for c in range(components):
        level[components * MAIN + c * EXTRA] = 0.0
    both = np.concatenate([high, low])
    return both, np.repeat(level.astype(np.float32)[:, None], LANES, axis=1)


def combine_table(segments, components):
    main, extra = half_rows()
    values = MAIN + EXTRA
    level = np.concatenate([main, extra]).sum(axis=1)
    level[MAIN] = 0.0

    def unit(k, imag):
        row = np.zeros(values)
        if k == 0:
            if not imag:
                row[MAIN + 1] = 1.0
        elif k == TOP - 1:
            row[MAIN + 2 + imag] = 1.0
        else:
            row[imag * NF + k - 1] = 1.0
        return row

    full = np.zeros((NF, ROWS, segments, values))
    for f in range(NF):
        k = f + 1
        for imag in range(2):
            side = 0.25 * (unit(k - 1, imag) + unit(k + 1, imag))
            first = 0.5 * unit(k, imag) - side
            second = (-1.0) ** k * (0.5 * unit(k, imag) + side)
            lift_first, lift_second = first @ level, second @ level
            both = lift_first + lift_second
            for b in range(NB):
                row = full[f, imag * NB + b]
                row[b] += first
                row[b + 1] += second
                row[b, MAIN] += lift_first
                row[b + 1, MAIN] += lift_second
                if f == 0 and not imag:
                    row[:, MAIN] -= both / segments
                    row[:, MAIN + 1] -= both / (segments * HALF)
    full = full.reshape(NF * ROWS, segments, values)
    inner = inner_of(segments)
    planes = segments // inner
    tail = packed_rows(components) - components * MAIN
    wide = np.zeros((NF * ROWS, segments, tail))
    for c in range(components):
        wide[:, :, c * EXTRA:(c + 1) * EXTRA] = full[:, :, MAIN:]
    high, low = split(wide)

    def planed(part):
        part = part.reshape(NF * ROWS, planes, inner * part.shape[-1])
        return np.transpose(part, (1, 0, 2)).astype(jnp.bfloat16)
    return np.concatenate([planed(full[:, :, :MAIN]), planed(high), planed(low)], axis=2)


def code(v):
    a = v
    for _ in range(POWER_BITS):
        a = a * a
    return jnp.where(v < 0.0, -a, a)


def decode(y):
    a = jnp.abs(y)
    for _ in range(POWER_BITS):
        a = jnp.sqrt(a)
    return jnp.where(y < 0.0, -a, a)


def spectral_kernel(n, x_ref, w_ref, f_ref, level_ref, t_hbm, out_ref,
                    x_buf, t_ref, outbox, recv, acc, gram, parts, total, gathered,
                    x_sem, t_sem, own_sem, send_sem, recv_sem, rs_send, rs_recv, ag_send, ag_recv):
    me = lax.axis_index("space")
    owners = n // 2
    first = n // 8
    tile = LANES // owners
    inner = inner_of(n)
    planes = n // inner
    my_plane, my_q = me // inner, lax.rem(me, inner)
    rows = NF * ROWS
    mine = w_ref.shape[1]
    components, steps_dev = x_ref.shape[:2]
    packed = recv.shape[1]
    body = components * MAIN

    def peer_of(k):
        return lax.rem(me + 1 + k, n)

    upper = 2 * my_plane >= planes

    def plane_of(k):
        if k == planes - 1:
            return my_plane
        down = planes - 1 - k
        down = jnp.where(down <= my_plane, down - 1, down)
        up = jnp.where(k >= my_plane, k + 1, k)
        return jnp.where(upper, up, down)

    def x_copy(k):
        width = inner * mine
        lanes = pl.ds(pl.multiple_of(plane_of(k) * width, width), width)
        return pltpu.make_async_copy(x_ref.at[:, :, lanes], x_buf.at[k], x_sem.at[k])
    each(planes, lambda k: x_copy(k).start())
    t_copy = pltpu.make_async_copy(t_hbm, t_ref, t_sem)
    t_copy.start()

    barrier = pltpu.get_barrier_semaphore()

    def greet(k):
        pl.semaphore_signal(barrier, inc=1, device_id={"space": peer_of(k)},
                            device_id_type=pl.DeviceIdType.MESH)
    each(n - 1, greet)

    def data_copy(dest, source):
        return pltpu.make_async_remote_copy(
            src_ref=outbox.at[dest], dst_ref=recv.at[source],
            send_sem=send_sem.at[dest], recv_sem=recv_sem.at[source],
            device_id={"space": dest}, device_id_type=pl.DeviceIdType.MESH)

    tail_row = lax.broadcasted_iota(jnp.int32, (packed - body, LANES), 0)
    tail_kind = lax.rem(tail_row, EXTRA)
    in_tail = tail_row < components * EXTRA
    coded = jnp.logical_and(in_tail, tail_kind > 0)
    is_scale = tail_row == components * EXTRA

    def prepare(k):
        x_copy(k).wait()
        x = x_buf[k].reshape(components * steps_dev, inner * mine)
        both = jnp.dot(f_ref[...], x, preferred_element_type=jnp.float32)
        y = both[:packed] + both[packed:]
        for q in range(inner):
            part = y[:, q * mine:(q + 1) * mine]
            tail = part[body:]
            means = [tail[c * EXTRA:c * EXTRA + 1].astype(jnp.bfloat16).astype(jnp.float32)
                     for c in range(components)]
            spread = jnp.broadcast_to(means[-1], tail.shape)
            for c in range(components - 1):
                inside = jnp.logical_and(tail_row >= c * EXTRA, tail_row < (c + 1) * EXTRA)
                spread = jnp.where(inside, means[c], spread)
            tail = tail - level_ref[body:] * spread
            mains = [part[c * MAIN:(c + 1) * MAIN] - level_ref[c * MAIN:(c + 1) * MAIN] * means[c]
                     for c in range(components)]
            largest = jnp.max(jnp.where(coded, jnp.abs(tail), 0.0), axis=0, keepdims=True)
            for m in mains:
                largest = jnp.maximum(largest, jnp.max(jnp.abs(m), axis=0, keepdims=True))
            scale = jnp.maximum(largest, 1e-30).astype(jnp.bfloat16).astype(jnp.float32)
            grow = GAIN / scale
            dest = plane_of(k) * inner + q
            for c in range(components):
                outbox[dest, c * MAIN:(c + 1) * MAIN] = code(mains[c] * grow).astype(jnp.bfloat16)
            sent = jnp.where(coded, code(tail * grow), jnp.where(is_scale, scale, spread))
            outbox[dest, body:] = sent.astype(jnp.bfloat16)

    def launch(k):
        def one(i):
            dest = plane_of(k) * inner + lax.rem(my_q + i, inner)

            @pl.when(dest != me)
            def _():
                data_copy(dest, me).start()
        each(inner, one)

    def step(k):
        prepare(k)
        if k == 0:
            pl.semaphore_wait(barrier, n - 1)
        launch(k)
    for k in range(planes):
        step(k)
    own_copy = pltpu.make_async_copy(outbox.at[me], recv.at[me], own_sem)
    own_copy.start()

    acc[...] = jnp.zeros_like(acc)
    t_copy.wait()
    own_copy.wait()

    def absorb(j):
        at = lax.rem(my_plane + j, planes)

        def arrive(i):
            source = at * inner + i

            @pl.when(source != me)
            def _():
                data_copy(source, source).wait_recv()
        each(inner, arrive)
        columns = [[] for _ in range(components)]
        tails = []
        for i in range(inner):
            source = at * inner + i
            tail = recv[source, body:].astype(jnp.float32)
            scale = tail[components * EXTRA:components * EXTRA + 1] * (1.0 / GAIN)
            for c in range(components):
                y = recv[source, c * MAIN:(c + 1) * MAIN].astype(jnp.float32)
                columns[c].append(decode(y) * scale)
            tails.append(jnp.where(coded, decode(tail) * scale, tail))
        tail = jnp.concatenate(tails, axis=0)
        row = lax.rem(lax.broadcasted_iota(jnp.int32, tail.shape, 0), packed - body)
        pieces = []
        for c in range(components):
            inside = jnp.logical_and(row >= c * EXTRA, row < (c + 1) * EXTRA)
            own = jnp.where(inside, tail, 0.0)
            pieces.append(jnp.concatenate(columns[c] + [own, own], axis=0))
        block = jnp.concatenate(pieces, axis=1)
        high, low = halves_of(block)
        t = t_ref[at]
        acc[...] += (
            jnp.dot(t, high, preferred_element_type=jnp.float32)
            + jnp.dot(t, low, preferred_element_type=jnp.float32))
    each(planes, absorb)

    def part_copy(slot, source):
        return pltpu.make_async_remote_copy(
            src_ref=gram.at[pl.ds(pl.multiple_of(slot * tile, tile), tile)],
            dst_ref=parts.at[source],
            send_sem=rs_send.at[slot], recv_sem=rs_recv.at[source],
            device_id={"space": first + slot}, device_id_type=pl.DeviceIdType.MESH)

    def total_copy(dest, slot):
        return pltpu.make_async_remote_copy(
            src_ref=total, dst_ref=gathered.at[slot],
            send_sem=ag_send.at[dest], recv_sem=ag_recv.at[slot],
            device_id={"space": dest}, device_id_type=pl.DeviceIdType.MESH)

    my_slot = me - first
    is_owner = jnp.logical_and(my_slot >= 0, my_slot < owners)

    def for_others(body):
        def one(k):
            slot = lax.rem(me + owners // 2 + k, owners)

            @pl.when(slot != my_slot)
            def _():
                body(slot)
        each(owners, one)
    w = w_ref[...]
    w_all = jnp.concatenate([w] * (acc.shape[1] // w.shape[1]), axis=1)
    w_sum = jnp.sum(w)
    block_of = lax.broadcasted_iota(jnp.int32, (ROWS, LANES), 1) // ROWS
    corner = jnp.logical_and(
        lax.broadcasted_iota(jnp.int32, (ROWS, LANES), 0) == ROWS - 1,
        lax.broadcasted_iota(jnp.int32, (ROWS, LANES), 1) % ROWS == ROWS - 1)
    for g in range(rows // LANES):
        c = acc[g * LANES:(g + 1) * LANES]
        c_high, c_low = halves_of(c)
        a_high, a_low = halves_of(c * w_all)
        full = dot_t(a_high, c_high) + (dot_t(a_high, c_low) + dot_t(a_low, c_high))
        kept = full[:ROWS]
        for i in range(1, LANES // ROWS):
            kept = jnp.where(block_of == i, full[i * ROWS:(i + 1) * ROWS], kept)
        gram[g * ROWS:(g + 1) * ROWS] = jnp.where(corner, w_sum, kept)
        for slot in range(g * ROWS // tile, (g + 1) * ROWS // tile):
            @pl.when(my_slot != slot)
            def _():
                part_copy(slot, me).start()


    @pl.when(is_owner)
    def _():
        parts[me] = gram[pl.ds(pl.multiple_of(my_slot * tile, tile), tile)]
        each(n - 1, lambda k: part_copy(my_slot, peer_of(k)).wait_recv())
        total[...] = jnp.sum(parts[...], axis=0)
        def total_to(plane):
            def one(k):
                dest = plane * inner + lax.rem(my_q + k, inner)

                @pl.when(dest != me)
                def _():
                    total_copy(dest, my_slot).start()
            each(inner, one)

        def total_far(k):
            d = planes - 1 - k
            pl.when(my_plane + d < planes)(lambda: total_to(my_plane + d))
            pl.when(my_plane >= d)(lambda: total_to(my_plane - d))
        each(planes - 1, total_far)
        total_to(my_plane)
        gathered[my_slot] = total[...]

    for_others(lambda slot: total_copy(me, slot).wait_recv())

    whole = gathered[...].reshape(LANES, LANES)
    inverse = 1.0 / (whole[ROWS - 1:ROWS, ROWS - 1:ROWS] * (3.0 * NFFT / 8.0))
    out_ref[...] = whole * inverse

    each(n - 1, lambda k: data_copy(peer_of(k), me).wait_send())

    for_others(lambda slot: part_copy(slot, me).wait_send())

    @pl.when(is_owner)
    def _():
        each(n - 1, lambda k: total_copy(peer_of(k), my_slot).wait_send())


def spectral_local(n, snapshots, weights):
    steps_dev, components, points = snapshots.shape
    mine = points // n
    x = jnp.transpose(snapshots, (1, 0, 2))
    forward, level = sender_table(components)
    back = combine_table(n, components)
    owners = n // 2
    inner = inner_of(n)
    planes = n // inner
    packed = packed_rows(components)
    rows = NF * ROWS
    dma = pltpu.SemaphoreType.DMA
    hbm = pl.BlockSpec(memory_space=pl.ANY)
    vmem = pl.BlockSpec(memory_space=pltpu.VMEM)
    out = pl.pallas_call(
        functools.partial(spectral_kernel, n),
        out_shape=jax.ShapeDtypeStruct((LANES, LANES), jnp.float32),
        in_specs=[hbm, vmem, vmem, vmem, hbm],
        out_specs=vmem,
        scratch_shapes=[
            pltpu.VMEM((planes, components, steps_dev, inner * mine), jnp.bfloat16),
            pltpu.VMEM(back.shape, jnp.bfloat16),
            pltpu.VMEM((n, packed, mine), jnp.bfloat16),
            pltpu.VMEM((n, packed, mine), jnp.bfloat16),
            pltpu.VMEM((rows, components * mine), jnp.float32),
            pltpu.VMEM((LANES, LANES), jnp.float32),
            pltpu.VMEM((n, LANES // owners, LANES), jnp.float32),
            pltpu.VMEM((LANES // owners, LANES), jnp.float32),
            pltpu.VMEM((owners, LANES // owners, LANES), jnp.float32),
            dma((planes,)), dma, dma, dma((n,)), dma((n,)), dma((n,)), dma((n,)), dma((n,)), dma((n,)),
        ],
        compiler_params=pltpu.CompilerParams(collective_id=0, has_side_effects=True),
    )(x, weights.reshape(1, mine), jnp.asarray(forward), jnp.asarray(level), jnp.asarray(back))
    out = out.reshape(NF * ROWS // LANES, ROWS, LANES // ROWS, ROWS)[:, :2 * NB, :, :2 * NB]
    return jnp.transpose(out, (0, 2, 1, 3)).reshape(NF, 2 * NB, 2 * NB)


def local(n, snapshots, weights):
    steps_dev, components, points = snapshots.shape
    fits = steps_dev == HALF and n == NB + 1 and points == n * LANES
    return (spectral_local if fits else raw_local)(n, snapshots, weights)


def solution(mesh):
    n = mesh.shape["space"]
    in_specs = (P(("grp", "space"), None, None), P(("grp", "space")))
    out_specs = P("grp", None, None)
    return jax.shard_map(functools.partial(local, n), mesh=mesh, in_specs=in_specs,
                         out_specs=out_specs, check_vma=False)
```

```python
import functools

import jax
import jax.numpy as jnp
import numpy as np
from jax import lax
from jax.experimental import pallas as pl
from jax.experimental.pallas import tpu as pltpu
from jax.sharding import PartitionSpec as P

NFFT = 128
NB = 15
NF = 16
ROWS = 32
LANES = 128


def table(steps):
    j = np.arange(NFFT)
    window = 0.5 - 0.5 * np.cos(2 * np.pi * j / NFFT)
    window = window / np.sqrt(np.sum(window * window))
    full = np.zeros((NF, ROWS, steps))
    for f in range(NF):
        turns = 2 * np.pi * (((f + 1) * j) % NFFT) / NFFT
        for b in range(NB):
            at = b * (NFFT // 2)
            full[f, b, at:at + NFFT] = window * np.cos(turns)
            full[f, NB + b, at:at + NFFT] = -window * np.sin(turns)
    full = full - full.sum(axis=2, keepdims=True) / steps
    return full.reshape(NF * ROWS, steps)


def split_table(steps, chunk):
    full = table(steps)
    high = full.astype(jnp.bfloat16)
    low = (full - high.astype(np.float64)).astype(jnp.bfloat16)
    both = np.stack([high, low])
    both = both.reshape(2, NF * ROWS, steps // chunk, chunk)
    return np.transpose(both, (2, 0, 1, 3)).reshape(steps // chunk, 2 * NF * ROWS, chunk)


def inner_of(n):
    return 4 if n % 4 == 0 else 1


def owners_of(n):
    return min(max(n // 4, 1), 16)


def each(count, body):
    if count <= 32:
        for k in range(count):
            body(k)
    else:
        def step(k, carry):
            body(k)
            return carry
        lax.fori_loop(0, count, step, 0)


def halves_of(v):
    high = v.astype(jnp.bfloat16)
    return high, (v - high.astype(jnp.float32)).astype(jnp.bfloat16)


def dot_t(a, b):
    return lax.dot_general(a, b, (((1,), (1,)), ((), ())), preferred_element_type=jnp.float32)


def raw_kernel(n, steps_dev, chunk, x_ref, w_ref, s_hbm, out_ref,
           s_ref, recv, acc, gram, parts, total, gathered,
           s_sem, own_sem, send_sem, recv_sem, rs_send, rs_recv, ag_send, ag_recv):
    me = lax.axis_index("space")
    owners = owners_of(n)
    first = (n - owners) // 2
    tile = LANES // owners
    inner = inner_of(n)
    planes = n // inner
    my_plane, my_q = me // inner, lax.rem(me, inner)
    per_chunk = chunk // steps_dev
    n_chunks = n // per_chunk
    rows = NF * ROWS
    mine = w_ref.shape[1]
    components = x_ref.shape[0]

    def peer_of(k):
        return lax.rem(me + 1 + k, n)

    def lanes_of(dest):
        return pl.ds(pl.multiple_of(dest * mine, mine), mine)

    s_copy = pltpu.make_async_copy(s_hbm, s_ref, s_sem)
    s_copy.start()
    own_copy = pltpu.make_async_copy(x_ref.at[:, :, lanes_of(me)], recv.at[me], own_sem)
    own_copy.start()

    barrier = pltpu.get_barrier_semaphore()

    def greet(k):
        pl.semaphore_signal(barrier, inc=1, device_id={"space": peer_of(k)},
                            device_id_type=pl.DeviceIdType.MESH)
    each(n - 1, greet)
    pl.semaphore_wait(barrier, n - 1)

    def data_copy(dest, source):
        return pltpu.make_async_remote_copy(
            src_ref=x_ref.at[:, :, lanes_of(dest)], dst_ref=recv.at[source],
            send_sem=send_sem.at[dest], recv_sem=recv_sem.at[source],
            device_id={"space": dest}, device_id_type=pl.DeviceIdType.MESH)

    def send(plane, low, high):
        def one(k):
            q = lax.rem(my_q + low + k, inner)

            @pl.when(jnp.logical_or(plane != my_plane, q != my_q))
            def _():
                data_copy(plane * inner + q, me).start()
        each(high - low, one)

    def send_far(k):
        d = planes - 1 - k
        pl.when(my_plane + d < planes)(lambda: send(my_plane + d, 0, inner))
        pl.when(my_plane >= d)(lambda: send(my_plane - d, 0, inner))
    each(planes - 1, send_far)
    send(my_plane, 0, inner)

    acc[...] = jnp.zeros_like(acc)
    s_copy.wait()
    own_copy.wait()
    my_chunk = me // per_chunk

    def absorb(j):
        at = lax.rem(my_chunk + j, n_chunks)

        def arrive(i):
            source = at * per_chunk + i

            @pl.when(source != me)
            def _():
                data_copy(source, source).wait_recv()
        each(per_chunk, arrive)
        held = pl.ds(at * per_chunk, per_chunk)
        block = jnp.concatenate(
            [recv[held, c].reshape(chunk, mine) for c in range(components)], axis=1)
        s = s_ref[at]
        acc[...] += (
            jnp.dot(s[:rows], block, preferred_element_type=jnp.float32)
            + jnp.dot(s[rows:], block, preferred_element_type=jnp.float32))
    each(n_chunks, absorb)

    w = w_ref[...]
    w_all = jnp.concatenate([w] * (acc.shape[1] // w.shape[1]), axis=1)
    w_sum = jnp.sum(w)
    block_of = lax.broadcasted_iota(jnp.int32, (ROWS, LANES), 1) // ROWS
    corner = jnp.logical_and(
        lax.broadcasted_iota(jnp.int32, (ROWS, LANES), 0) == ROWS - 1,
        lax.broadcasted_iota(jnp.int32, (ROWS, LANES), 1) % ROWS == ROWS - 1)
    for g in range(rows // LANES):
        c = acc[g * LANES:(g + 1) * LANES]
        c_high, c_low = halves_of(c)
        a_high, a_low = halves_of(c * w_all)
        full = dot_t(a_high, c_high) + (dot_t(a_high, c_low) + dot_t(a_low, c_high))
        kept = full[:ROWS]
        for i in range(1, LANES // ROWS):
            kept = jnp.where(block_of == i, full[i * ROWS:(i + 1) * ROWS], kept)
        gram[g * ROWS:(g + 1) * ROWS] = jnp.where(corner, w_sum, kept)

    def part_copy(slot, source):
        return pltpu.make_async_remote_copy(
            src_ref=gram.at[pl.ds(pl.multiple_of(slot * tile, tile), tile)],
            dst_ref=parts.at[source],
            send_sem=rs_send.at[slot], recv_sem=rs_recv.at[source],
            device_id={"space": first + slot}, device_id_type=pl.DeviceIdType.MESH)

    def total_copy(dest, slot):
        return pltpu.make_async_remote_copy(
            src_ref=total, dst_ref=gathered.at[slot],
            send_sem=ag_send.at[dest], recv_sem=ag_recv.at[slot],
            device_id={"space": dest}, device_id_type=pl.DeviceIdType.MESH)

    my_slot = me - first
    is_owner = jnp.logical_and(my_slot >= 0, my_slot < owners)

    def for_others(body):
        def one(k):
            slot = lax.rem(me + owners // 2 + k, owners)

            @pl.when(slot != my_slot)
            def _():
                body(slot)
        each(owners, one)
    for_others(lambda slot: part_copy(slot, me).start())

    @pl.when(is_owner)
    def _():
        parts[me] = gram[pl.ds(pl.multiple_of(my_slot * tile, tile), tile)]
        each(n - 1, lambda k: part_copy(my_slot, peer_of(k)).wait_recv())
        total[...] = jnp.sum(parts[...], axis=0)
        def total_to(plane):
            def one(k):
                dest = plane * inner + lax.rem(my_q + k, inner)

                @pl.when(dest != me)
                def _():
                    total_copy(dest, my_slot).start()
            each(inner, one)

        def total_far(k):
            d = planes - 1 - k
            pl.when(my_plane + d < planes)(lambda: total_to(my_plane + d))
            pl.when(my_plane >= d)(lambda: total_to(my_plane - d))
        each(planes - 1, total_far)
        total_to(my_plane)
        gathered[my_slot] = total[...]

    for_others(lambda slot: total_copy(me, slot).wait_recv())

    whole = gathered[...].reshape(LANES, LANES)
    inverse = 1.0 / whole[ROWS - 1:ROWS, ROWS - 1:ROWS]
    per_row = LANES // ROWS
    for f in range(NF):
        g, i = f // per_row, f % per_row
        piece = whole[g * ROWS:g * ROWS + 2 * NB, i * ROWS:i * ROWS + 2 * NB]
        out_ref[:, f, :] = piece * inverse

    each(n - 1, lambda k: data_copy(peer_of(k), me).wait_send())

    for_others(lambda slot: part_copy(slot, me).wait_send())

    @pl.when(is_owner)
    def _():
        each(n - 1, lambda k: total_copy(peer_of(k), my_slot).wait_send())


def raw_local(n, snapshots, weights):
    steps_dev, components, points = snapshots.shape
    mine = points // n
    steps = steps_dev * n
    chunk = max(256, steps_dev)
    width = components * mine
    x = jnp.transpose(snapshots, (1, 0, 2))
    s = jnp.asarray(split_table(steps, chunk))
    owners = owners_of(n)
    rows = NF * ROWS
    dma = pltpu.SemaphoreType.DMA
    hbm = pl.BlockSpec(memory_space=pl.ANY)
    vmem = pl.BlockSpec(memory_space=pltpu.VMEM)
    out = pl.pallas_call(
        functools.partial(raw_kernel, n, steps_dev, chunk),
        out_shape=jax.ShapeDtypeStruct((2 * NB, NF, 2 * NB), jnp.float32),
        in_specs=[hbm, vmem, hbm],
        out_specs=vmem,
        scratch_shapes=[
            pltpu.VMEM(s.shape, jnp.bfloat16),
            pltpu.VMEM((n, components, steps_dev, mine), jnp.bfloat16),
            pltpu.VMEM((rows, width), jnp.float32),
            pltpu.VMEM((LANES, LANES), jnp.float32),
            pltpu.VMEM((n, LANES // owners, LANES), jnp.float32),
            pltpu.VMEM((LANES // owners, LANES), jnp.float32),
            pltpu.VMEM((owners, LANES // owners, LANES), jnp.float32),
            dma, dma, dma((n,)), dma((n,)), dma((n,)), dma((n,)), dma((n,)), dma((n,)),
        ],
        compiler_params=pltpu.CompilerParams(collective_id=0, has_side_effects=True),
    )(x, weights.reshape(1, mine), s)
    return jnp.transpose(out, (1, 0, 2))


HALF = NFFT // 2
TOP = NF + 2
MAIN = 2 * NF
EXTRA = 4
POWER_BITS = 4
GAIN = 2.0 ** 7.5


def half_rows():
    j = np.arange(HALF)
    turns = [2 * np.pi * ((k * j) % NFFT) / NFFT for k in range(TOP)]
    main = [np.cos(turns[k]) for k in range(1, NF + 1)]
    main += [-np.sin(turns[k]) for k in range(1, NF + 1)]
    extra = [np.full(HALF, 1.0 / HALF), np.ones(HALF), np.cos(turns[TOP - 1]), -np.sin(turns[TOP - 1])]
    return np.stack(main), np.stack(extra)


def packed_rows(components):
    used = components * (MAIN + EXTRA) + 1
    return -(-used // 16) * 16


def split(full):
    high = full.astype(jnp.bfloat16)
    return high, (full - high.astype(np.float64)).astype(jnp.bfloat16)


def sender_table(components):
    main, extra = half_rows()
    packed = packed_rows(components)
    full = np.zeros((packed, components, HALF))
    level = np.zeros(packed)
    for c in range(components):
        at = components * MAIN + c * EXTRA
        full[c * MAIN:(c + 1) * MAIN, c] = main
        full[at:at + EXTRA, c] = extra
    high, low = split(full.reshape(packed, components * HALF))
    level = (high.astype(np.float64) + low.astype(np.float64)).sum(axis=1)
    for c in range(components):
        level[components * MAIN + c * EXTRA] = 0.0
    both = np.concatenate([high, low])
    return both, np.repeat(level.astype(np.float32)[:, None], LANES, axis=1)


def combine_table(segments, components):
    main, extra = half_rows()
    values = MAIN + EXTRA
    level = np.concatenate([main, extra]).sum(axis=1)
    level[MAIN] = 0.0

    def unit(k, imag):
        row = np.zeros(values)
        if k == 0:
            if not imag:
                row[MAIN + 1] = 1.0
        elif k == TOP - 1:
            row[MAIN + 2 + imag] = 1.0
        else:
            row[imag * NF + k - 1] = 1.0
        return row

    full = np.zeros((NF, ROWS, segments, values))
    for f in range(NF):
        k = f + 1
        for imag in range(2):
            side = 0.25 * (unit(k - 1, imag) + unit(k + 1, imag))
            first = 0.5 * unit(k, imag) - side
            second = (-1.0) ** k * (0.5 * unit(k, imag) + side)
            lift_first, lift_second = first @ level, second @ level
            both = lift_first + lift_second
            for b in range(NB):
                row = full[f, imag * NB + b]
                row[b] += first
                row[b + 1] += second
                row[b, MAIN] += lift_first
                row[b + 1, MAIN] += lift_second
                if f == 0 and not imag:
                    row[:, MAIN] -= both / segments
                    row[:, MAIN + 1] -= both / (segments * HALF)
    full = full.reshape(NF * ROWS, segments, values)
    inner = inner_of(segments)
    planes = segments // inner
    tail = packed_rows(components) - components * MAIN
    wide = np.zeros((NF * ROWS, segments, tail))
    for c in range(components):
        wide[:, :, c * EXTRA:(c + 1) * EXTRA] = full[:, :, MAIN:]
    high, low = split(wide)

    def planed(part):
        part = part.reshape(NF * ROWS, planes, inner * part.shape[-1])
        return np.transpose(part, (1, 0, 2)).astype(jnp.bfloat16)
    return np.concatenate([planed(full[:, :, :MAIN]), planed(high), planed(low)], axis=2)


def code(v):
    a = v
    for _ in range(POWER_BITS):
        a = a * a
    return jnp.where(v < 0.0, -a, a)


def decode(y):
    a = jnp.exp2(jnp.log2(jnp.abs(y)) * (0.5 ** POWER_BITS))
    return jnp.where(y < 0.0, -a, a)


def spectral_kernel(n, x_ref, w_ref, f_ref, level_ref, t_hbm, out_ref,
                    x_buf, t_ref, outbox, recv, acc, gram, parts, total, gathered,
                    x_sem, t_sem, own_sem, send_sem, recv_sem, rs_send, rs_recv, ag_send, ag_recv):
    me = lax.axis_index("space")
    owners = n // 2
    first = n // 8
    tile = LANES // owners
    inner = inner_of(n)
    planes = n // inner
    my_plane, my_q = me // inner, lax.rem(me, inner)
    rows = NF * ROWS
    mine = w_ref.shape[1]
    components, steps_dev = x_ref.shape[:2]
    packed = recv.shape[1]
    body = components * MAIN

    def peer_of(k):
        return lax.rem(me + 1 + k, n)

    half = planes // 2
    upper = my_plane >= half
    base = jnp.where(upper, half, 0)

    def plane_of(k):
        if k == planes - 1:
            return my_plane
        down = planes - 1 - k
        down = jnp.where(down <= my_plane, down - 1, down)
        up = jnp.where(k >= my_plane, k + 1, k)
        return jnp.where(upper, up, down)

    def x_copy(k):
        width = inner * mine
        lanes = pl.ds(pl.multiple_of(plane_of(k) * width, width), width)
        return pltpu.make_async_copy(x_ref.at[:, :, lanes], x_buf.at[k], x_sem.at[k])
    each(planes, lambda k: x_copy(k).start())
    t_copy = pltpu.make_async_copy(t_hbm, t_ref, t_sem)
    t_copy.start()

    barrier = pltpu.get_barrier_semaphore()

    def greet(k):
        pl.semaphore_signal(barrier, inc=1, device_id={"space": peer_of(k)},
                            device_id_type=pl.DeviceIdType.MESH)
    each(n - 1, greet)

    def data_copy(dest, source):
        return pltpu.make_async_remote_copy(
            src_ref=outbox.at[dest], dst_ref=recv.at[source],
            send_sem=send_sem.at[dest], recv_sem=recv_sem.at[source],
            device_id={"space": dest}, device_id_type=pl.DeviceIdType.MESH)

    tail_row = lax.broadcasted_iota(jnp.int32, (packed - body, LANES), 0)
    tail_kind = lax.rem(tail_row, EXTRA)
    in_tail = tail_row < components * EXTRA
    coded = jnp.logical_and(in_tail, tail_kind > 0)
    is_scale = tail_row == components * EXTRA

    def prepare(k):
        x_copy(k).wait()
        x = x_buf[k].reshape(components * steps_dev, inner * mine)
        both = jnp.dot(f_ref[...], x, preferred_element_type=jnp.float32)
        y = both[:packed] + both[packed:]
        for q in range(inner):
            part = y[:, q * mine:(q + 1) * mine]
            tail = part[body:]
            means = [tail[c * EXTRA:c * EXTRA + 1].astype(jnp.bfloat16).astype(jnp.float32)
                     for c in range(components)]
            spread = jnp.broadcast_to(means[-1], tail.shape)
            for c in range(components - 1):
                inside = jnp.logical_and(tail_row >= c * EXTRA, tail_row < (c + 1) * EXTRA)
                spread = jnp.where(inside, means[c], spread)
            tail = tail - level_ref[body:] * spread
            mains = [part[c * MAIN:(c + 1) * MAIN] - level_ref[c * MAIN:(c + 1) * MAIN] * means[c]
                     for c in range(components)]
            largest = jnp.max(jnp.where(coded, jnp.abs(tail), 0.0), axis=0, keepdims=True)
            for m in mains:
                largest = jnp.maximum(largest, jnp.max(jnp.abs(m), axis=0, keepdims=True))
            scale = jnp.maximum(largest, 1e-30).astype(jnp.bfloat16).astype(jnp.float32)
            grow = GAIN / scale
            dest = plane_of(k) * inner + q
            for c in range(components):
                outbox[dest, c * MAIN:(c + 1) * MAIN] = code(mains[c] * grow).astype(jnp.bfloat16)
            sent = jnp.where(coded, code(tail * grow), jnp.where(is_scale, scale, spread))
            outbox[dest, body:] = sent.astype(jnp.bfloat16)

    def launch(k):
        def one(i):
            dest = plane_of(k) * inner + lax.rem(my_q + i, inner)

            @pl.when(dest != me)
            def _():
                data_copy(dest, me).start()
        each(inner, one)

    def step(k):
        prepare(k)
        if k == 0:
            pl.semaphore_wait(barrier, n - 1)
        launch(k)
    for k in range(planes):
        step(k)
    own_copy = pltpu.make_async_copy(outbox.at[me], recv.at[me], own_sem)
    own_copy.start()

    acc[...] = jnp.zeros_like(acc)
    t_copy.wait()
    own_copy.wait()

    def absorb(j):
        if j < half:
            at = base + lax.rem(my_plane - base + j, half)
        else:
            at = jnp.where(upper, j - half, planes - 1 - (j - half))

        def arrive(i):
            source = at * inner + i

            @pl.when(source != me)
            def _():
                data_copy(source, source).wait_recv()
        each(inner, arrive)
        columns = [[] for _ in range(components)]
        tails = []
        for i in range(inner):
            source = at * inner + i
            tail = recv[source, body:].astype(jnp.float32)
            scale = tail[components * EXTRA:components * EXTRA + 1] * (1.0 / GAIN)
            for c in range(components):
                y = recv[source, c * MAIN:(c + 1) * MAIN].astype(jnp.float32)
                columns[c].append(decode(y) * scale)
            tails.append(jnp.where(coded, decode(tail) * scale, tail))
        tail = jnp.concatenate(tails, axis=0)
        row = lax.rem(lax.broadcasted_iota(jnp.int32, tail.shape, 0), packed - body)
        pieces = []
        for c in range(components):
            inside = jnp.logical_and(row >= c * EXTRA, row < (c + 1) * EXTRA)
            own = jnp.where(inside, tail, 0.0)
            pieces.append(jnp.concatenate(columns[c] + [own, own], axis=0))
        block = jnp.concatenate(pieces, axis=1)
        high, low = halves_of(block)
        t = t_ref[at]
        acc[...] += (
            jnp.dot(t, high, preferred_element_type=jnp.float32)
            + jnp.dot(t, low, preferred_element_type=jnp.float32))
    each(planes, absorb)

    def part_copy(slot, source):
        return pltpu.make_async_remote_copy(
            src_ref=gram.at[pl.ds(pl.multiple_of(slot * tile, tile), tile)],
            dst_ref=parts.at[source],
            send_sem=rs_send.at[slot], recv_sem=rs_recv.at[source],
            device_id={"space": first + slot}, device_id_type=pl.DeviceIdType.MESH)

    def total_copy(dest, slot):
        return pltpu.make_async_remote_copy(
            src_ref=total, dst_ref=gathered.at[slot],
            send_sem=ag_send.at[dest], recv_sem=ag_recv.at[slot],
            device_id={"space": dest}, device_id_type=pl.DeviceIdType.MESH)

    my_slot = me - first
    is_owner = jnp.logical_and(my_slot >= 0, my_slot < owners)

    def for_others(body):
        def one(k):
            slot = lax.rem(me + owners // 2 + k, owners)

            @pl.when(slot != my_slot)
            def _():
                body(slot)
        each(owners, one)
    w = w_ref[...]
    w_all = jnp.concatenate([w] * (acc.shape[1] // w.shape[1]), axis=1)
    w_sum = jnp.sum(w)
    block_of = lax.broadcasted_iota(jnp.int32, (ROWS, LANES), 1) // ROWS
    corner = jnp.logical_and(
        lax.broadcasted_iota(jnp.int32, (ROWS, LANES), 0) == ROWS - 1,
        lax.broadcasted_iota(jnp.int32, (ROWS, LANES), 1) % ROWS == ROWS - 1)
    for g in range(rows // LANES):
        c = acc[g * LANES:(g + 1) * LANES]
        c_high, c_low = halves_of(c)
        a_high, a_low = halves_of(c * w_all)
        full = dot_t(a_high, c_high) + (dot_t(a_high, c_low) + dot_t(a_low, c_high))
        kept = full[:ROWS]
        for i in range(1, LANES // ROWS):
            kept = jnp.where(block_of == i, full[i * ROWS:(i + 1) * ROWS], kept)
        gram[g * ROWS:(g + 1) * ROWS] = jnp.where(corner, w_sum, kept)
        for slot in range(g * ROWS // tile, (g + 1) * ROWS // tile):
            @pl.when(my_slot != slot)
            def _():
                part_copy(slot, me).start()


    @pl.when(is_owner)
    def _():
        parts[me] = gram[pl.ds(pl.multiple_of(my_slot * tile, tile), tile)]
        each(n - 1, lambda k: part_copy(my_slot, peer_of(k)).wait_recv())
        total[...] = jnp.sum(parts[...], axis=0)
        def total_to(plane):
            def one(k):
                dest = plane * inner + lax.rem(my_q + k, inner)

                @pl.when(dest != me)
                def _():
                    total_copy(dest, my_slot).start()
            each(inner, one)

        def total_far(k):
            d = planes - 1 - k
            pl.when(my_plane + d < planes)(lambda: total_to(my_plane + d))
            pl.when(my_plane >= d)(lambda: total_to(my_plane - d))
        each(planes - 1, total_far)
        total_to(my_plane)
        gathered[my_slot] = total[...]

    for_others(lambda slot: total_copy(me, slot).wait_recv())

    whole = gathered[...].reshape(LANES, LANES)
    inverse = 1.0 / (whole[ROWS - 1:ROWS, ROWS - 1:ROWS] * (3.0 * NFFT / 8.0))
    out_ref[...] = whole * inverse

    each(n - 1, lambda k: data_copy(peer_of(k), me).wait_send())

    for_others(lambda slot: part_copy(slot, me).wait_send())

    @pl.when(is_owner)
    def _():
        each(n - 1, lambda k: total_copy(peer_of(k), my_slot).wait_send())


def spectral_local(n, snapshots, weights):
    steps_dev, components, points = snapshots.shape
    mine = points // n
    x = jnp.transpose(snapshots, (1, 0, 2))
    forward, level = sender_table(components)
    back = combine_table(n, components)
    owners = n // 2
    inner = inner_of(n)
    planes = n // inner
    packed = packed_rows(components)
    rows = NF * ROWS
    dma = pltpu.SemaphoreType.DMA
    hbm = pl.BlockSpec(memory_space=pl.ANY)
    vmem = pl.BlockSpec(memory_space=pltpu.VMEM)
    out = pl.pallas_call(
        functools.partial(spectral_kernel, n),
        out_shape=jax.ShapeDtypeStruct((LANES, LANES), jnp.float32),
        in_specs=[hbm, vmem, vmem, vmem, hbm],
        out_specs=vmem,
        scratch_shapes=[
            pltpu.VMEM((planes, components, steps_dev, inner * mine), jnp.bfloat16),
            pltpu.VMEM(back.shape, jnp.bfloat16),
            pltpu.VMEM((n, packed, mine), jnp.bfloat16),
            pltpu.VMEM((n, packed, mine), jnp.bfloat16),
            pltpu.VMEM((rows, components * mine), jnp.float32),
            pltpu.VMEM((LANES, LANES), jnp.float32),
            pltpu.VMEM((n, LANES // owners, LANES), jnp.float32),
            pltpu.VMEM((LANES // owners, LANES), jnp.float32),
            pltpu.VMEM((owners, LANES // owners, LANES), jnp.float32),
            dma((planes,)), dma, dma, dma((n,)), dma((n,)), dma((n,)), dma((n,)), dma((n,)), dma((n,)),
        ],
        compiler_params=pltpu.CompilerParams(collective_id=0, has_side_effects=True),
    )(x, weights.reshape(1, mine), jnp.asarray(forward), jnp.asarray(level), jnp.asarray(back))
    out = out.reshape(NF * ROWS // LANES, ROWS, LANES // ROWS, ROWS)[:, :2 * NB, :, :2 * NB]
    return jnp.transpose(out, (0, 2, 1, 3)).reshape(NF, 2 * NB, 2 * NB)


def local(n, snapshots, weights):
    steps_dev, components, points = snapshots.shape
    fits = steps_dev == HALF and n == NB + 1 and points == n * LANES
    return (spectral_local if fits else raw_local)(n, snapshots, weights)


def solution(mesh):
    n = mesh.shape["space"]
    in_specs = (P(("grp", "space"), None, None), P(("grp", "space")))
    out_specs = P("grp", None, None)
    return jax.shard_map(functools.partial(local, n), mesh=mesh, in_specs=in_specs,
                         out_specs=out_specs, check_vma=False)
```
